128 devices in a mesh: grp: 64 (over z, y, x), tp: 2 (over core).
Axes of the slice: x: 4, y: 4, z: 4, core: 2. Of those that a mesh axis runs over, the one named last changes fastest.
Arguments:
- hidden_in: bfloat16 [4096, 2, 2560], P('grp'), may hold values from -6 to 6
- prompt_len: int32 [48], replicated, may hold values from 1 to 32768, as said below
- slot_req: int32 [64], replicated, may hold values from 0 to 47, as said below
- sample_req: int32 [4096, 1], P('grp'), may hold values from 0 to 47; in each aligned block of 64 rows (0 to 63, 64 to 127, ...) at most 2 rows name the same one
- tail_len: int32 [4096], P('grp'), may hold values from 0 to 256
- slot_kv: bfloat16 [64, 8, 2, 80, 2048], P('grp', 'tp'), may hold values from -60 to 60
- tail_kv: bfloat16 [4096, 8, 2, 80, 256], P('grp', 'tp'), may hold values from -6 to 6
- attn_gain: float32 [2560], replicated, may hold values from 0.5 to 1.5
- wqkv: bfloat16 [2560, 3840], P(None, 'tp'), may hold values from -0.25 to 0.25
- wo: bfloat16 [2560, 2560], P('tp'), may hold values from -0.125 to 0.125
- out_gain: float32 [2560], replicated, may hold values from 0.5 to 1.5
- score_w: float32 [2560], replicated, may hold values from -0.125 to 0.125
Outputs:
- hidden_out: float32 [4096, 2, 2560], P('grp', None, 'tp')
- row_score: float32 [4096, 2], P('grp')
The draws below stay inside these ranges and needn't reach their ends.
Inputs may be any that keep to these rules, and one draw needn't show every extreme that they name: `prompt_len`: exactly 16 prompts are longer than 2048 tokens. `slot_req`: a prompt of at most 2048 tokens owns one slot, a longer one two. `sample_req`: among the samples of one index of grp no prompt appears more than 2 times.
All inputs are finite; a program needn't handle non-finite values.
Results may differ from the reference program's by a relative error of at most 0.012.
Values may be sent and summed in bfloat16 or wider, within the bound.
A program may use at most 192 MiB of HBM per device.

```python
import math
import jax
import jax.numpy as jnp
import numpy as np
from jax import lax

D = 2560
H = 32
KVH = 8
HD = 80
W = 4096
QPK = 4
SLOT = 2048
PMAX = 32768
TMAX = 256
SPG = 64
REQS = 48
LONGS = 16
MOST = 2
SAMPLES = 4096
N_GRP = 64


def slot_layout(key):
    base_key = jax.random.fold_in(key, 7)
    key_order, key_long, key_len_long, key_len_short = jax.random.split(base_key, 4)
    rank_long = jax.random.permutation(key_long, REQS).astype(jnp.int32)
    is_long = rank_long < LONGS
    long_ids = jnp.argsort(rank_long)[:LONGS].astype(jnp.int32)
    owners = jnp.concatenate([jnp.arange(REQS, dtype=jnp.int32), long_ids])
    order = jax.random.permutation(key_order, N_GRP)
    slot_owner = owners[order].astype(jnp.int32)
    long_len = jax.random.randint(key_len_long, (REQS,), SLOT + 1, PMAX + 1)
    short_len = jax.random.randint(key_len_short, (REQS,), 1, SLOT + 1)
    lengths = jnp.where(is_long, long_len, short_len)
    lengths = jnp.where(rank_long == 0, PMAX, lengths)
    lengths = jnp.where(rank_long == LONGS, SLOT, lengths)
    return (slot_owner, lengths.astype(jnp.int32))


def draw_prompt_len(key, part):
    return slot_layout(key)[1]


def draw_slot_req(key, part):
    return slot_layout(key)[0]


def draw_tail_len(key, part):
    key_vals, key_spot = jax.random.split(jax.random.fold_in(key, 5))
    counts = jax.random.randint(key_vals, (SAMPLES,), 0, TMAX + 1)
    spot = jax.random.randint(key_spot, (), 0, SAMPLES)
    counts = jnp.where(jnp.arange(SAMPLES) == spot, TMAX, counts)
    return counts.astype(jnp.int32)


def draw_slot_kv(key, part):
    shape = (N_GRP, KVH, 2, HD, SLOT)
    key_base = jax.random.fold_in(jax.random.fold_in(key, 3), 0)
    values = jnp.clip(1.2 * jax.random.normal(key_base, shape, jnp.float32), -6.0, 6.0)
    return values.astype(jnp.bfloat16)


def steps_of(key, extent, cuts, low, top_value):
    loudness, own = 1.0, jax.random.fold_in(key, 6)
    for dim, blocks in cuts:
        draws = jnp.exp(jax.random.uniform(jax.random.fold_in(own, dim), (blocks,), jnp.float32, low / len(cuts), top_value / len(cuts)))
        loudness = loudness * jnp.repeat(draws, extent[dim] // blocks).reshape([-1 if axis == dim else 1 for axis in range(len(extent))])
    return loudness


def routed_block(rng, own, number, rows, amount, top, limit, slope):
    sequence = jax.random.permutation(rng, amount)
    heavy_load, usual = portions_of(amount, rows * top, limit, slope, True), portions_of(amount, rows * top, limit, slope, False)
    places = jnp.arange(amount)

    def named(tallies, rotation):
        used = int((tallies > 0).sum())
        fixed = max(1, used // 4)
        shifted = fixed + (places - fixed + rotation * (used - fixed)) % max(1, amount - fixed)
        return jnp.zeros((amount,), jnp.int32).at[sequence[jnp.where(places < fixed, places, shifted)]].set(jnp.asarray(tallies, jnp.int32))

    tallies = jnp.where(number % 4 == 0, named(heavy_load, number // 4), named(usual, number - number // 4 - 1))
    mixed = jax.random.permutation(jax.random.fold_in(own, 3), amount)
    donor, receiver = mixed[0:amount // 2 * 2:2], mixed[1:amount // 2 * 2:2]
    slack = jnp.minimum(tallies[donor] - 1, limit - tallies[receiver]) // 2
    slack = jnp.where((donor == sequence[0]) | (receiver == sequence[0]) | (tallies[receiver] == 0), 0, jnp.maximum(slack, 0))
    shifted = jax.random.randint(jax.random.fold_in(own, 4), (amount // 2,), 0, 1 << 20) % (slack + 1)
    tallies = tallies.at[donor].add(-shifted).at[receiver].add(shifted)
    members = jnp.searchsorted(jnp.cumsum(tallies), jnp.arange(rows * top), side="right").astype(jnp.int32)
    table = members.reshape(top, rows).T
    table = table[jax.random.permutation(jax.random.fold_in(own, 1), rows)]
    rotation = jax.random.randint(jax.random.fold_in(own, 2), (rows, 1), 0, top)
    return jnp.take_along_axis(table, (jnp.arange(top)[None, :] + rotation) % top, axis=1)


def portions_of(amount, total, bound, lean, full):
    weights = [(1 << 20) // math.isqrt(grade ** lean) + 1 for grade in range(1, amount + 1)]
    largest = bound if full else min(bound, max(-(-total // amount), total * weights[0] // sum(weights)))
    least = 1 if total - largest >= amount - 1 else 0
    holding, spare = [largest] + [least] * (amount - 1), total - largest - least * (amount - 1)
    while spare > 0:
        candidates = [i for i in range(1, amount) if holding[i] < largest] or [i for i in range(1, amount) if holding[i] < bound]
        mass, remaining = sum([weights[i] for i in candidates]), spare
        for i in candidates:
            addition = min(bound - holding[i], max(1, remaining * weights[i] // mass), spare)
            holding[i] = holding[i] + addition
            spare = spare - addition
    return np.array(holding)


def normal_values(key, dims, spread, reach, shards=(), held_as=jnp.bfloat16):
    drawn = spread * jax.random.normal(key, dims, jnp.float32)
    if shards:
        drawn = drawn * steps_of(key, dims, shards, -0.22, 0.18)
    return jnp.clip(drawn, -reach, reach).astype(held_as)


def setup_inputs(seed: int = 0) -> dict:
    keys = jax.random.split(jax.random.key(seed), 13)
    hidden_in = normal_values(keys[0], (SAMPLES, 2, D), 1.0, 6.0, ((0, 64),))
    prompt_len = draw_prompt_len(jax.random.fold_in(keys[12], 71), 0)
    slot_req = draw_slot_req(jax.random.fold_in(keys[12], 71), 0)
    sample_req_keys = jax.random.split(jax.random.fold_in(keys[3], 1), SAMPLES // SPG)
    sample_req_turns = jax.random.permutation(jax.random.fold_in(keys[3], 3), SAMPLES // SPG)
    sample_req = jax.vmap(lambda own, number: routed_block(jax.random.fold_in(keys[3], 2), own, number, SPG, REQS, 1, MOST, 2))(sample_req_keys, sample_req_turns).reshape((SAMPLES, 1))
    tail_len = draw_tail_len(jax.random.fold_in(keys[12], 71), 0)
    slot_kv = draw_slot_kv(jax.random.fold_in(keys[12], 71), 0)
    tail_kv = normal_values(keys[6], (SAMPLES, KVH, 2, HD, TMAX), 1.2, 6.0, ((0, 64), (1, 2)))
    attn_gain = jnp.clip(1.0 + 0.1 * jax.random.normal(keys[7], (D,), jnp.float32), 0.5, 1.5)
    wqkv = normal_values(keys[8], (D, KVH * (QPK + 2) * HD), (D // 4) ** -0.5, 0.25, ((1, 2),))
    wo = normal_values(keys[9], (H * HD, D), (H * HD) ** -0.5, 0.125, ((0, 2),))
    out_gain = jnp.clip(1.0 + 0.1 * jax.random.normal(keys[10], (D,), jnp.float32), 0.5, 1.5)
    score_w = normal_values(keys[11], (D,), D ** -0.5, 0.125, (), jnp.float32)
    return {"hidden_in": hidden_in, "prompt_len": prompt_len, "slot_req": slot_req, "sample_req": sample_req, "tail_len": tail_len, "slot_kv": slot_kv, "tail_kv": tail_kv, "attn_gain": attn_gain, "wqkv": wqkv, "wo": wo, "out_gain": out_gain, "score_w": score_w}


epsilon = 1e-05
rope_base = 10000.0

def rope_pair(positions, head_dim):
    half_dim = head_dim // 2
    frequency = rope_base ** (-jnp.arange(half_dim, dtype=jnp.float32) / half_dim)
    angles = positions.astype(jnp.float32)[..., None] * frequency
    angles = jnp.concatenate([angles, angles], axis=-1)
    return (jnp.cos(angles), jnp.sin(angles))

def rotate(vectors, cosine, sine):
    half_dim = vectors.shape[-1] // 2
    turned = jnp.concatenate([-vectors[..., half_dim:], vectors[..., :half_dim]], axis=-1)
    return vectors * cosine + turned * sine

def reference(hidden_in, prompt_len, slot_req, sample_req, tail_len, slot_kv, tail_kv, attn_gain, wqkv, wo, out_gain, score_w):
    flat_in = hidden_in.reshape(SAMPLES * 2, D).astype(jnp.float32)
    normed = (flat_in * lax.rsqrt(lax.optimization_barrier(jnp.mean(flat_in * flat_in, axis=-1, keepdims=True)) + epsilon) * attn_gain).astype(jnp.bfloat16)
    projected = jnp.dot(normed, wqkv, preferred_element_type=jnp.float32).reshape(SAMPLES, 2, KVH, QPK + 2, HD)
    my_reqs = sample_req[:, 0].astype(jnp.int32)
    lengths = prompt_len[my_reqs]
    positions = lengths[:, None] + tail_len[:, None] + jnp.arange(2, dtype=jnp.int32)[None, :]
    cosine, sine = rope_pair(positions, HD)
    query_new = rotate(projected[:, :, :, :QPK], cosine[:, :, None, None, :], sine[:, :, None, None, :]).astype(jnp.bfloat16)
    key_new = rotate(projected[:, :, :, QPK], cosine[:, :, None, :], sine[:, :, None, :]).astype(jnp.bfloat16)
    value_new = projected[:, :, :, QPK + 1].astype(jnp.bfloat16)
    slot_ids = jnp.arange(N_GRP, dtype=jnp.int32)
    owns = slot_req[None, :] == jnp.arange(REQS, dtype=jnp.int32)[:, None]
    first_slot = lax.optimization_barrier(jnp.min(jnp.where(owns, slot_ids[None, :], N_GRP), axis=1)).astype(jnp.int32)
    second_slot = lax.optimization_barrier(jnp.max(jnp.where(owns, slot_ids[None, :], -1), axis=1)).astype(jnp.int32)
    score_scale = HD ** (-0.5)

    def attend(items):
        request, length, tail_count, queries, own_keys, own_values, tail_cache = items
        prompt = jnp.concatenate([slot_kv[first_slot[request]], slot_kv[second_slot[request]]], axis=-1)
        cached = jnp.minimum(length, W)
        prompt_index = jnp.arange(2 * SLOT, dtype=jnp.int32)
        prompt_pos = length - cached + prompt_index
        prompt_ok = prompt_index < cached
        tail_index = jnp.arange(TMAX, dtype=jnp.int32)
        tail_pos = length + tail_index
        tail_ok = tail_index < tail_count
        own_pos = length + tail_count + jnp.arange(2, dtype=jnp.int32)
        key_all = jnp.concatenate([prompt[:, 0], tail_cache[:, 0], own_keys.transpose(1, 2, 0)], axis=-1).astype(jnp.float32)
        value_all = jnp.concatenate([prompt[:, 1], tail_cache[:, 1], own_values.transpose(1, 2, 0)], axis=-1).astype(jnp.float32)
        key_pos = jnp.concatenate([prompt_pos, tail_pos, own_pos])
        key_ok = jnp.concatenate([prompt_ok, tail_ok, jnp.ones((2,), dtype=bool)])
        allowed = key_ok[None, :] & (key_pos[None, :] <= own_pos[:, None]) & (key_pos[None, :] >= own_pos[:, None] - W + 1)
        scores = jnp.einsum('tkjh,khn->tkjn', queries.astype(jnp.float32), key_all) * score_scale
        scores = jnp.where(allowed[:, None, None, :], scores, -jnp.inf)
        highest = lax.optimization_barrier(jnp.max(scores, axis=-1, keepdims=True))
        weights = jnp.exp(scores - highest)
        totals = lax.optimization_barrier(jnp.sum(weights, axis=-1))
        rounded = lax.optimization_barrier(weights.astype(jnp.bfloat16)).astype(jnp.float32)
        output = jnp.einsum('tkjn,khn->tkjh', rounded, value_all) / totals[..., None]
        return output.astype(jnp.bfloat16)
    outputs = lax.map(attend, (my_reqs, lengths, tail_len, query_new, key_new, value_new, tail_kv), batch_size=16)
    attention = outputs.reshape(SAMPLES * 2, H * HD)
    mixed = jnp.dot(attention, wo, preferred_element_type=jnp.float32)
    residual = flat_in + mixed
    hidden_out = residual.reshape(SAMPLES, 2, D)
    mean_square = lax.optimization_barrier(jnp.mean(residual * residual, axis=-1))
    row_score = lax.optimization_barrier(jnp.sum(residual * out_gain * score_w, axis=-1)) * lax.rsqrt(mean_square + epsilon)
    return (hidden_out, row_score.reshape(SAMPLES, 2))
```

```python
import functools

import jax
import jax.numpy as jnp
import numpy as np
from jax import lax
from jax.experimental import pallas as pl
from jax.experimental.pallas import tpu as pltpu
from jax.sharding import PartitionSpec as P

W = 4096
HD = 80
EPS = 1e-05
ROPE_BASE = 10000.0
NEG = -1e30
MESH = pl.DeviceIdType.MESH
F32 = jnp.float32
BF16 = jnp.bfloat16
LOG2E = 1.4426950408889634
SCALE2 = HD**-0.5 * LOG2E
WIDE = 384
SIDE = 320


def iota(shape, dim):
    return lax.broadcasted_iota(jnp.int32, shape, dim)


def to_row(col, size):
    eye = iota((size, size), 0) == iota((size, size), 1)
    return jnp.sum(jnp.where(eye, col, 0.0), axis=0, keepdims=True)


def to_col(row, size):
    eye = iota((size, size), 0) == iota((size, size), 1)
    return jnp.sum(jnp.where(eye, row, 0.0), axis=1, keepdims=True)


def split3(x):
    hi = x.astype(BF16).astype(F32)
    rest = x - hi
    mid = rest.astype(BF16).astype(F32)
    low = (rest - mid).astype(BF16).astype(F32)
    return hi, mid, low


def sample_codes(req, rank_scale, samples):
    req_row = to_row(req, samples)
    shape = (samples, samples)
    before = (req == req_row) & (iota(shape, 1) < iota(shape, 0))
    rank = jnp.sum(jnp.where(before, 1.0, 0.0), axis=1, keepdims=True)
    return req * rank_scale + rank


def qkv_kernel(
    x_ref, req_ref, tail_ref, plen_ref, slot_ref, gain_ref, freq_ref, w_ref,
    send_ref, qt_ref, qb_ref, own_ref, normed, acc,
):
    step = pl.program_id(0)
    last = pl.num_programs(0) - 1
    n = x_ref.shape[0]
    d = x_ref.shape[1] // 2
    chunks, _, width = normed.shape

    @pl.when(step == 0)
    def _():
        for t in range(2):
            x = x_ref[:, t * d : (t + 1) * d].astype(F32)
            r = lax.rsqrt(jnp.mean(x * x, axis=-1, keepdims=True) + EPS)
            y = (x * r * gain_ref[...]).astype(BF16)
            for c in range(chunks):
                normed[c, t * n : (t + 1) * n, :] = y[:, c * width : (c + 1) * width]

    part = jnp.dot(normed[step], w_ref[...], preferred_element_type=F32)

    @pl.when(step == 0)
    def _():
        acc[...] = part

    @pl.when(step > 0)
    def _():
        acc[...] += part

    @pl.when(step == last)
    def _():
        req = req_ref[...].astype(F32)
        plen = plen_ref[...].astype(F32)
        reqs = plen.shape[1]
        slots = slot_ref.shape[1]
        owned = req == iota((n, reqs), 1).astype(F32)
        length = jnp.sum(jnp.where(owned, plen, 0.0), axis=1, keepdims=True)
        tail = to_col(tail_ref[...].astype(F32), n)
        pos = length + tail
        pos = jnp.concatenate([pos, pos + 1.0], axis=0)
        angle = pos * freq_ref[...]
        cosine = jnp.cos(angle)
        sine = jnp.sin(angle)
        half = HD // 2
        sine = jnp.where(iota(sine.shape, 1) < half, -sine, sine)

        def rope(u):
            turned = jnp.concatenate([u[:, half:], u[:, :half]], axis=1)
            return u * cosine + turned * sine

        own_ref[...] = jnp.zeros_like(own_ref)
        for k in range(4):
            base = k * 6 * HD
            for j in range(4):
                u = rope(acc[:, base + j * HD : base + (j + 1) * HD]).astype(BF16)
                for t in range(2):
                    row = (t * 4 + j) * n
                    qb_ref[row : row + n, k * HD : (k + 1) * HD] = u[t * n : (t + 1) * n]
            key = rope(acc[:, base + 4 * HD : base + 5 * HD]).astype(BF16).astype(F32)
            value = acc[:, base + 5 * HD : base + 6 * HD].astype(BF16).astype(F32)
            for t in range(2):
                own_ref[t, :, k * HD : (k + 1) * HD] = key[t * n : (t + 1) * n]
                own_ref[2 + t, :, k * HD : (k + 1) * HD] = value[t * n : (t + 1) * n]
        side = jnp.broadcast_to(tail, (n, WIDE - SIDE)).astype(BF16)
        for tj in range(8):
            qb_ref[tj * n : (tj + 1) * n, SIDE:] = side

        code = sample_codes(req, 2.0, n)
        cols = 8 * n
        rows = slots * 16
        spread = iota((n, cols), 0) == (iota((n, cols), 1) & (n - 1))
        code_row = jnp.sum(jnp.where(spread, code, 0.0), axis=0, keepdims=True)
        spread = iota((rows, slots), 1) == (iota((rows, slots), 0) >> 4)
        slot = slot_ref[...].astype(F32)
        slot_col = jnp.sum(jnp.where(spread, slot, 0.0), axis=1, keepdims=True)
        item = ((iota((rows, 1), 0) >> 3) & 1).astype(F32)
        want = slot_col * 2.0 + item
        pick = (want == code_row) & (
            (iota((rows, cols), 0) & 7) == (iota((rows, cols), 1) // n)
        )
        pick = jnp.where(pick, 1.0, 0.0).astype(BF16)
        packed = qb_ref[...]
        send_ref[...] = jnp.dot(pick, packed, preferred_element_type=F32).astype(BF16)
        r = iota((cols, cols), 0)
        c = iota((cols, cols), 1)
        perm = ((r >> 3) == (c & (n - 1))) & ((r & 7) == (c // n))
        perm = jnp.where(perm, 1.0, 0.0).astype(BF16)
        qt_ref[...] = jnp.dot(perm, packed, preferred_element_type=F32)


def qkv(x, req, tail, plen, slot, gain, freq, w):
    n = x.shape[0]
    d = x.shape[1] // 2
    chunks = 5
    width = d // chunks
    slots = slot.shape[1]
    full = lambda a: pl.BlockSpec(a.shape, lambda i: (0,) * a.ndim)
    whole = lambda *s: pl.BlockSpec(s, lambda i: (0,) * len(s))
    return pl.pallas_call(
        qkv_kernel,
        grid=(chunks,),
        in_specs=[full(a) for a in (x, req, tail, plen, slot, gain, freq)]
        + [pl.BlockSpec((width, w.shape[1]), lambda i: (i, 0))],
        out_specs=[
            whole(slots * 16, WIDE), whole(8 * n, WIDE), whole(8 * n, WIDE), whole(4, n, WIDE),
        ],
        out_shape=[
            jax.ShapeDtypeStruct((slots * 16, WIDE), BF16),
            jax.ShapeDtypeStruct((8 * n, WIDE), F32),
            jax.ShapeDtypeStruct((8 * n, WIDE), BF16),
            jax.ShapeDtypeStruct((4, n, WIDE), F32),
        ],
        scratch_shapes=[
            pltpu.VMEM((chunks, 2 * n, width), BF16),
            pltpu.VMEM((2 * n, w.shape[1]), F32),
        ],
        compiler_params=pltpu.CompilerParams(vmem_limit_bytes=60 << 20),
        name="qkv",
    )(x, req, tail, plen, slot, gain, freq, w)


def exchange_kernel(groups, rows, s_ref, r_ref, send_sem, recv_sem, own_sem):
    me = lax.axis_index("grp")
    barrier = pltpu.get_barrier_semaphore()

    def greet(d, _):
        peer = lax.rem(me + d, groups)
        pl.semaphore_signal(barrier, inc=1, device_id={"grp": peer}, device_id_type=MESH)
        return 0

    lax.fori_loop(1, groups, greet, 0)

    def block(ref, i):
        return ref.at[pl.ds(pl.multiple_of(i * rows, rows), rows)]

    own = pltpu.make_async_copy(block(s_ref, me), block(r_ref, me), own_sem)
    own.start()
    pl.semaphore_wait(barrier, groups - 1)

    def copy_to(d):
        peer = lax.rem(me + d, groups)
        return pltpu.make_async_remote_copy(
            src_ref=block(s_ref, peer),
            dst_ref=block(r_ref, me),
            send_sem=send_sem.at[d],
            recv_sem=recv_sem.at[d],
            device_id={"grp": peer},
            device_id_type=MESH,
        )

    def send(d, _):
        copy_to(d).start()
        return 0

    def finish(d, _):
        copy_to(d).wait()
        return 0

    lax.fori_loop(1, groups, send, 0)
    lax.fori_loop(1, groups, finish, 0)
    own.wait()


def exchange(s, groups, number):
    rows = s.shape[0] // groups
    return pl.pallas_call(
        functools.partial(exchange_kernel, groups, rows),
        out_shape=jax.ShapeDtypeStruct(s.shape, s.dtype),
        in_specs=[pl.BlockSpec(memory_space=pl.ANY)],
        out_specs=pl.BlockSpec(memory_space=pl.ANY),
        scratch_shapes=[
            pltpu.SemaphoreType.DMA((groups,)),
            pltpu.SemaphoreType.DMA((groups,)),
            pltpu.SemaphoreType.DMA,
        ],
        compiler_params=pltpu.CompilerParams(collective_id=number, has_side_effects=True),
        name="exchange" + str(number),
    )(s)


def store_side(ref, rows, logs):
    n = logs[0].shape[0]
    lane = iota((n, WIDE - SIDE), 1)
    side = jnp.where(lane == 12, 1.0, 0.0)
    for k, value in enumerate(logs):
        for p, term in enumerate(split3(value)):
            side = jnp.where(lane == 4 * p + k, term, side)
    ref[rows, SIDE:] = side.astype(ref.dtype)


def tail_kernel(q_ref, kv_ref, o_ref):
    n = kv_ref.shape[0]
    length = kv_ref.shape[4]
    scores = []
    limits = []
    for s in range(n):
        limit = q_ref[s * 8 : (s + 1) * 8, SIDE : SIDE + 1]
        for k in range(4):
            q = q_ref[s * 8 : (s + 1) * 8, k * HD : (k + 1) * HD].astype(BF16)
            scores.append(jnp.dot(q, kv_ref[s, k, 0], preferred_element_type=F32))
            limits.append(limit)
    score = jnp.concatenate(scores, axis=0) * SCALE2
    limit = jnp.concatenate(limits, axis=0)
    at = iota(score.shape, 1).astype(F32)
    score = jnp.where(at < limit, score, NEG)
    top = jnp.max(score, axis=1, keepdims=True)
    weight = jnp.exp2(score - top)
    total = jnp.sum(weight, axis=1, keepdims=True)
    inverse = 1.0 / total
    logs = top + jnp.log2(total)
    weight = weight.astype(BF16)
    for s in range(n):
        rows = slice(s * 8, (s + 1) * 8)
        parts = []
        for k in range(4):
            at = slice((s * 4 + k) * 8, (s * 4 + k + 1) * 8)
            out = lax.dot_general(
                weight[at], kv_ref[s, k, 1], (((1,), (1,)), ((), ())),
                preferred_element_type=F32,
            )
            o_ref[rows, k * HD : (k + 1) * HD] = out * inverse[at]
            parts.append(logs[at])
        store_side(o_ref, rows, parts)


def tail_attention(qt, kv):
    n = kv.shape[0]
    step = 8
    return pl.pallas_call(
        tail_kernel,
        grid=(n // step,),
        in_specs=[
            pl.BlockSpec((step * 8, WIDE), lambda i: (i, 0)),
            pl.BlockSpec((step,) + kv.shape[1:], lambda i: (i, 0, 0, 0, 0)),
        ],
        out_specs=pl.BlockSpec((step * 8, WIDE), lambda i: (i, 0)),
        out_shape=jax.ShapeDtypeStruct((n * 8, WIDE), F32),
        compiler_params=pltpu.CompilerParams(vmem_limit_bytes=60 << 20),
        name="tail",
    )(qt, kv)


def slot_kernel(q_ref, kv_ref, slot_ref, plen_ref, o_ref):
    rows = q_ref.shape[0]
    length = kv_ref.shape[4]
    slots = slot_ref.shape[1]
    reqs = plen_ref.shape[1]
    me = lax.axis_index("grp")
    slot = slot_ref[...].astype(F32)
    at = iota((1, slots), 1)
    mine = jnp.sum(jnp.where(at == me, slot, 0.0), axis=1, keepdims=True)
    part = jnp.sum(jnp.where((slot == mine) & (at < me), 1.0, 0.0), axis=1, keepdims=True)
    owned = iota((1, reqs), 1).astype(F32) == mine
    tokens = jnp.sum(jnp.where(owned, plen_ref[...].astype(F32), 0.0), axis=1, keepdims=True)
    cached = jnp.minimum(tokens, float(W))
    start = part * float(length)
    index = iota((1, length), 1).astype(F32)
    bias = jnp.where(index < cached - start, 0.0, NEG)
    sub = 128
    near = 384
    for b in range(rows // sub):
        span = slice(b * sub, (b + 1) * sub)
        tail = q_ref[span, SIDE : SIDE + 128 - SIDE % 128].astype(F32)[:, 0:1]
        token = ((iota((sub, 1), 0) >> 2) & 1).astype(F32)
        floor = tail + token + (cached - float(W)) - start
        logs = []
        for k in range(4):
            q = q_ref[span, k * HD : (k + 1) * HD]
            score = jnp.dot(q, kv_ref[0, k, 0], preferred_element_type=F32)
            score = score * SCALE2 + bias
            head = jnp.where(index[:, :near] > floor, score[:, :near], NEG)
            score = jnp.concatenate([head, score[:, near:]], axis=1)
            top = jnp.max(score, axis=1, keepdims=True)
            weight = jnp.exp2(score - top)
            total = jnp.sum(weight, axis=1, keepdims=True)
            out = lax.dot_general(
                weight.astype(BF16), kv_ref[0, k, 1], (((1,), (1,)), ((), ())),
                preferred_element_type=F32,
            )
            o_ref[span, k * HD : (k + 1) * HD] = (out * (1.0 / total)).astype(BF16)
            logs.append(top + jnp.log2(total))
        store_side(o_ref, span, logs)


def slot_attention(r, kv, slot, plen):
    rows = r.shape[0]
    step = min(rows, 256)
    full = lambda a: pl.BlockSpec(a.shape, lambda i: (0,) * a.ndim)
    return pl.pallas_call(
        slot_kernel,
        grid=(rows // step,),
        in_specs=[pl.BlockSpec((step, WIDE), lambda i: (i, 0)), full(kv), full(slot), full(plen)],
        out_specs=pl.BlockSpec((step, WIDE), lambda i: (i, 0)),
        out_shape=jax.ShapeDtypeStruct((rows, WIDE), BF16),
        compiler_params=pltpu.CompilerParams(vmem_limit_bytes=60 << 20),
        name="slot",
    )(r, kv, slot, plen)


def mix_kernel(b_ref, t_ref, qb_ref, own_ref, req_ref, slot_ref, wo_ref, m_ref, mb_ref, att):
    @pl.when(pl.program_id(0) == 0)
    def _():
        n = own_ref.shape[1]
        slots = slot_ref.shape[1]
        rows = 8 * n
        back = slots * 16
        code = sample_codes(req_ref[...].astype(F32), 4.0, n)
        spread = iota((rows, n), 1) == (iota((rows, n), 0) & (n - 1))
        code = jnp.sum(jnp.where(spread, to_row(code, n), 0.0), axis=1, keepdims=True)
        slot = slot_ref[...].astype(F32)
        slot_col = to_col(slot, slots)
        earlier = (slot == slot_col) & (iota((slots, slots), 1) < iota((slots, slots), 0))
        part = jnp.sum(jnp.where(earlier, 1.0, 0.0), axis=1, keepdims=True)
        key = slot_col * 4.0 + part * 2.0
        spread = iota((slots, back), 0) == (iota((slots, back), 1) >> 4)
        key = jnp.sum(jnp.where(spread, key, 0.0), axis=0, keepdims=True)
        key = key + ((iota((1, back), 1) >> 3) & 1).astype(F32)
        same = (iota((rows, back), 0) // n) == (iota((rows, back), 1) & 7)
        code = jnp.where(same, code, -8.0)
        returned = b_ref[...]
        parts = []
        for p in range(2):
            pick = jnp.where(key == code + 2.0 * p, 1.0, 0.0).astype(BF16)
            parts.append(jnp.dot(pick, returned, preferred_element_type=F32))
        r = iota((rows, rows), 0)
        c = iota((rows, rows), 1)
        perm = ((c >> 3) == (r & (n - 1))) & ((c & 7) == (r // n))
        perm = jnp.where(perm, 1.0, 0.0).astype(BF16)
        parts.append(jnp.dot(perm, t_ref[...].astype(BF16), preferred_element_type=F32))

        l = iota((WIDE, 128), 0)
        c = iota((WIDE, 128), 1)
        gather = (l >= SIDE) & (l < SIDE + 12) & (((l - SIDE) & 3) == c)
        gather = jnp.where(gather, 1.0, 0.0).astype(BF16)
        segment = jnp.where((l // HD == c) & (c < 4), 1.0, 0.0)
        logs = [jnp.dot(x.astype(BF16), gather, preferred_element_type=F32) for x in parts]
        logs[1] = jnp.where(parts[1][:, SIDE + 12 : SIDE + 13] > 0.5, logs[1], NEG)
        query = qb_ref[...].astype(F32)
        values = [x for x in parts]
        for u in range(2):
            keys = jnp.concatenate([own_ref[u]] * 8, axis=0)
            s = jnp.dot(
                query * keys, segment, preferred_element_type=F32,
                precision=lax.Precision.HIGHEST,
            ) * SCALE2
            if u:
                s = jnp.where(iota(s.shape, 0) >= 4 * n, s, NEG)
            logs.append(s)
            values.append(jnp.concatenate([own_ref[2 + u]] * 8, axis=0))
        top = functools.reduce(jnp.maximum, logs)
        weights = [jnp.exp2(x - top) for x in logs]
        inverse = 1.0 / functools.reduce(jnp.add, weights)
        lane = iota((rows, WIDE), 1)
        out = jnp.zeros((rows, WIDE), F32)
        for w, v in zip(weights, values):
            w = w * inverse
            wide = jnp.broadcast_to(w[:, 3:4], (rows, WIDE))
            for k in (2, 1, 0):
                wide = jnp.where(lane < (k + 1) * HD, w[:, k : k + 1], wide)
            out += wide * v
        out = out.astype(BF16)
        for k in range(4):
            for j in range(4):
                for t in range(2):
                    row = (t * 4 + j) * n
                    att[t * n : (t + 1) * n, (k * 4 + j) * HD : (k * 4 + j + 1) * HD] = out[
                        row : row + n, k * HD : (k + 1) * HD
                    ]

    mixed = jnp.dot(att[...], wo_ref[...], preferred_element_type=F32)
    m_ref[...] = mixed
    mb_ref[...] = mixed.astype(BF16)


def mix(b, t, qb, own, req, slot, wo):
    n = own.shape[1]
    d = wo.shape[1]
    width = 512
    full = lambda a: pl.BlockSpec(a.shape, lambda i: (0,) * a.ndim)
    return pl.pallas_call(
        mix_kernel,
        grid=(d // width,),
        in_specs=[full(a) for a in (b, t, qb, own, req, slot)]
        + [pl.BlockSpec((wo.shape[0], width), lambda i: (0, i))],
        out_specs=[pl.BlockSpec((2 * n, width), lambda i: (0, i))] * 2,
        out_shape=[
            jax.ShapeDtypeStruct((2 * n, d), F32),
            jax.ShapeDtypeStruct((2 * n, d), BF16),
        ],
        scratch_shapes=[pltpu.VMEM((2 * n, wo.shape[0]), BF16)],
        compiler_params=pltpu.CompilerParams(vmem_limit_bytes=60 << 20),
        name="mix",
    )(b, t, qb, own, req, slot, wo)


def finish_kernel(m_ref, mb_ref, x_ref, gain_ref, w_ref, h_ref, s_ref, got, send_sem, recv_sem):
    tp = lax.axis_index("tp")
    partner = {"tp": 1 - tp}
    barrier = pltpu.get_barrier_semaphore()
    pl.semaphore_signal(barrier, inc=1, device_id=partner, device_id_type=MESH)
    pl.semaphore_wait(barrier, 1)
    copy = pltpu.make_async_remote_copy(
        src_ref=mb_ref, dst_ref=got, send_sem=send_sem, recv_sem=recv_sem,
        device_id=partner, device_id_type=MESH,
    )
    copy.start()
    n = x_ref.shape[0]
    d = x_ref.shape[1] // 2
    share = d // 2
    scale = gain_ref[...] * w_ref[...]
    copy.wait()
    mine = pl.multiple_of(tp * share, 128)
    for t in range(2):
        rows = slice(t * n, (t + 1) * n)
        total = (
            x_ref[:, t * d : (t + 1) * d].astype(F32) + m_ref[rows, :] + got[rows, :].astype(F32)
        )
        square = jnp.mean(total * total, axis=-1, keepdims=True)
        score = jnp.sum(total * scale, axis=-1, keepdims=True) * lax.rsqrt(square + EPS)
        s_ref[:, t : t + 1] = score
        at = pl.multiple_of(tp * share + t * d, 128)
        h_ref[:, t * share : (t + 1) * share] = (
            x_ref[:, pl.ds(at, share)].astype(F32)
            + m_ref[rows, pl.ds(mine, share)]
            + got[rows, pl.ds(mine, share)].astype(F32)
        )


def finish(m, mb, x, gain, w):
    n = x.shape[0]
    d = x.shape[1] // 2
    vmem = pl.BlockSpec(memory_space=pltpu.VMEM)
    return pl.pallas_call(
        finish_kernel,
        in_specs=[vmem] * 5,
        out_specs=[vmem] * 2,
        out_shape=[
            jax.ShapeDtypeStruct((n, d), F32),
            jax.ShapeDtypeStruct((n, 2), F32),
        ],
        scratch_shapes=[
            pltpu.VMEM((2 * n, d), BF16),
            pltpu.SemaphoreType.DMA,
            pltpu.SemaphoreType.DMA,
        ],
        compiler_params=pltpu.CompilerParams(collective_id=7, has_side_effects=True),
        name="finish",
    )(m, mb, x, gain, w)


def local(
    hidden_in, prompt_len, slot_req, sample_req, tail_len, slot_kv, tail_kv,
    attn_gain, wqkv, wo, out_gain, score_w,
):
    n, _, d = hidden_in.shape
    groups = lax.axis_size("grp")
    x = hidden_in.reshape(n, 2 * d)
    tail = tail_len.reshape(1, n)
    plen = prompt_len.reshape(1, -1)
    slot = slot_req.reshape(1, -1)
    half = HD // 2
    freq = ROPE_BASE ** (-np.arange(half, dtype=np.float64) / half)
    freq = jnp.asarray(np.concatenate([freq, freq])[None, :], F32)
    send, qt, qb, own = qkv(x, sample_req, tail, plen, slot, attn_gain.reshape(1, d), freq, wqkv)
    got = exchange(send, groups, 0)
    tails = tail_attention(qt, tail_kv)
    part = slot_attention(got, slot_kv, slot, plen)
    back = exchange(part, groups, 1)
    m, mb = mix(back, tails, qb, own, sample_req, slot, wo)
    h, score = finish(m, mb, x, out_gain.reshape(1, d), score_w.reshape(1, d))
    return (h.reshape(n, 2, d // 2), score)


def solution(mesh):
    in_specs = (
        P("grp", None, None),
        P(),
        P(),
        P("grp", None),
        P("grp"),
        P("grp", "tp", None, None, None),
        P("grp", "tp", None, None, None),
        P(),
        P(None, "tp"),
        P("tp", None),
        P(),
        P(),
    )
    out_specs = (P("grp", None, "tp"), P("grp", None))
    return jax.shard_map(local, mesh=mesh, in_specs=in_specs, out_specs=out_specs, check_vma=False)
```

```python
import functools

import jax
import jax.numpy as jnp
import numpy as np
from jax import lax
from jax.experimental import pallas as pl
from jax.experimental.pallas import tpu as pltpu
from jax.sharding import PartitionSpec as P

W = 4096
HD = 80
EPS = 1e-05
ROPE_BASE = 10000.0
NEG = -1e30
MESH = pl.DeviceIdType.MESH
F32 = jnp.float32
BF16 = jnp.bfloat16
LOG2E = 1.4426950408889634
SCALE2 = HD**-0.5 * LOG2E
WIDE = 384
SIDE = 320


def iota(shape, dim):
    return lax.broadcasted_iota(jnp.int32, shape, dim)


def to_row(col, size):
    eye = iota((size, size), 0) == iota((size, size), 1)
    return jnp.sum(jnp.where(eye, col, 0.0), axis=0, keepdims=True)


def to_col(row, size):
    eye = iota((size, size), 0) == iota((size, size), 1)
    return jnp.sum(jnp.where(eye, row, 0.0), axis=1, keepdims=True)


def split3(x):
    hi = x.astype(BF16).astype(F32)
    rest = x - hi
    mid = rest.astype(BF16).astype(F32)
    low = (rest - mid).astype(BF16).astype(F32)
    return hi, mid, low


def sample_codes(req, rank_scale, samples):
    req_row = to_row(req, samples)
    shape = (samples, samples)
    before = (req == req_row) & (iota(shape, 1) < iota(shape, 0))
    rank = jnp.sum(jnp.where(before, 1.0, 0.0), axis=1, keepdims=True)
    return req * rank_scale + rank


def qkv_kernel(
    x_ref, req_ref, tail_ref, plen_ref, slot_ref, gain_ref, freq_ref, w_ref,
    send_ref, qt_ref, qb_ref, own_ref, normed, acc,
):
    step = pl.program_id(0)
    last = pl.num_programs(0) - 1
    n = x_ref.shape[0]
    d = x_ref.shape[1] // 2
    chunks, _, width = normed.shape

    @pl.when(step == 0)
    def _():
        for t in range(2):
            x = x_ref[:, t * d : (t + 1) * d].astype(F32)
            r = lax.rsqrt(jnp.mean(x * x, axis=-1, keepdims=True) + EPS)
            y = (x * r * gain_ref[...]).astype(BF16)
            for c in range(chunks):
                normed[c, t * n : (t + 1) * n, :] = y[:, c * width : (c + 1) * width]

    part = jnp.dot(normed[step], w_ref[...], preferred_element_type=F32)

    @pl.when(step == 0)
    def _():
        acc[...] = part

    @pl.when(step > 0)
    def _():
        acc[...] += part

    @pl.when(step == last)
    def _():
        req = to_col(req_ref[...].astype(F32), n)
        plen = plen_ref[...].astype(F32)
        reqs = plen.shape[1]
        slots = slot_ref.shape[1]
        owned = req == iota((n, reqs), 1).astype(F32)
        length = jnp.sum(jnp.where(owned, plen, 0.0), axis=1, keepdims=True)
        tail = to_col(tail_ref[...].astype(F32), n)
        pos = length + tail
        pos = jnp.concatenate([pos, pos + 1.0], axis=0)
        angle = pos * freq_ref[...]
        cosine = jnp.cos(angle)
        sine = jnp.sin(angle)
        half = HD // 2
        sine = jnp.where(iota(sine.shape, 1) < half, -sine, sine)

        def rope(u):
            turned = jnp.concatenate([u[:, half:], u[:, :half]], axis=1)
            return u * cosine + turned * sine

        own_ref[...] = jnp.zeros_like(own_ref)
        for k in range(4):
            base = k * 6 * HD
            for j in range(4):
                u = (rope(acc[:, base + j * HD : base + (j + 1) * HD]) * SCALE2).astype(BF16)
                for t in range(2):
                    row = (t * 4 + j) * n
                    qb_ref[row : row + n, k * HD : (k + 1) * HD] = u[t * n : (t + 1) * n]
            key = rope(acc[:, base + 4 * HD : base + 5 * HD]).astype(BF16).astype(F32)
            value = acc[:, base + 5 * HD : base + 6 * HD].astype(BF16).astype(F32)
            for t in range(2):
                own_ref[t, :, k * HD : (k + 1) * HD] = key[t * n : (t + 1) * n]
                own_ref[2 + t, :, k * HD : (k + 1) * HD] = value[t * n : (t + 1) * n]
        side = jnp.broadcast_to(tail, (n, WIDE - SIDE)).astype(BF16)
        for tj in range(8):
            qb_ref[tj * n : (tj + 1) * n, SIDE:] = side

        code = sample_codes(req, 2.0, n)
        cols = 8 * n
        rows = slots * 16
        spread = iota((n, cols), 0) == (iota((n, cols), 1) & (n - 1))
        code_row = jnp.sum(jnp.where(spread, code, 0.0), axis=0, keepdims=True)
        spread = iota((rows, slots), 1) == (iota((rows, slots), 0) >> 4)
        slot = slot_ref[...].astype(F32)
        slot_col = jnp.sum(jnp.where(spread, slot, 0.0), axis=1, keepdims=True)
        item = ((iota((rows, 1), 0) >> 3) & 1).astype(F32)
        want = slot_col * 2.0 + item
        pick = (want == code_row) & (
            (iota((rows, cols), 0) & 7) == (iota((rows, cols), 1) // n)
        )
        pick = jnp.where(pick, 1.0, 0.0).astype(BF16)
        packed = qb_ref[...]
        send_ref[...] = jnp.dot(pick, packed, preferred_element_type=F32).astype(BF16)
        r = iota((cols, cols), 0)
        c = iota((cols, cols), 1)
        perm = ((r >> 3) == (c & (n - 1))) & ((r & 7) == (c // n))
        perm = jnp.where(perm, 1.0, 0.0).astype(BF16)
        qt_ref[...] = jnp.dot(perm, packed, preferred_element_type=F32)


def qkv(x, req, tail, plen, slot, gain, freq, w):
    n = x.shape[0]
    d = x.shape[1] // 2
    chunks = 5
    width = d // chunks
    slots = slot.shape[1]
    full = lambda a: pl.BlockSpec(a.shape, lambda i: (0,) * a.ndim)
    whole = lambda *s: pl.BlockSpec(s, lambda i: (0,) * len(s))
    return pl.pallas_call(
        qkv_kernel,
        grid=(chunks,),
        in_specs=[full(a) for a in (x, req, tail, plen, slot, gain, freq)]
        + [pl.BlockSpec((width, w.shape[1]), lambda i: (i, 0))],
        out_specs=[
            whole(slots * 16, WIDE), whole(8 * n, WIDE), whole(8 * n, WIDE), whole(4, n, WIDE),
        ],
        out_shape=[
            jax.ShapeDtypeStruct((slots * 16, WIDE), BF16),
            jax.ShapeDtypeStruct((8 * n, WIDE), F32),
            jax.ShapeDtypeStruct((8 * n, WIDE), BF16),
            jax.ShapeDtypeStruct((4, n, WIDE), F32),
        ],
        scratch_shapes=[
            pltpu.VMEM((chunks, 2 * n, width), BF16),
            pltpu.VMEM((2 * n, w.shape[1]), F32),
        ],
        compiler_params=pltpu.CompilerParams(vmem_limit_bytes=60 << 20),
        name="qkv",
    )(x, req, tail, plen, slot, gain, freq, w)


def store_side(ref, rows, logs):
    n = logs[0].shape[0]
    lane = iota((n, WIDE - SIDE), 1)
    side = jnp.where(lane == 12, 1.0, 0.0)
    for k, value in enumerate(logs):
        for p, term in enumerate(split3(value)):
            side = jnp.where(lane == 4 * p + k, term, side)
    ref[rows, SIDE:] = side.astype(ref.dtype)


def tail_block(q_ref, kv_ref, o_ref, base):
    n = kv_ref.shape[0]
    scores = []
    limits = []
    for s in range(n):
        rows = pl.ds(pl.multiple_of(base + s * 8, 8), 8)
        limit = q_ref[rows, SIDE:][:, 0:1]
        for k in range(4):
            q = q_ref[rows, k * HD : (k + 1) * HD].astype(BF16)
            scores.append(jnp.dot(q, kv_ref[s, k, 0], preferred_element_type=F32))
            limits.append(limit)
    score = jnp.concatenate(scores, axis=0)
    limit = jnp.concatenate(limits, axis=0)
    at = iota(score.shape, 1).astype(F32)
    score = jnp.where(at < limit, score, NEG)
    top = jnp.max(score, axis=1, keepdims=True)
    weight = jnp.exp2(score - top)
    total = jnp.sum(weight, axis=1, keepdims=True)
    inverse = 1.0 / total
    logs = top + jnp.log2(total)
    weight = weight.astype(BF16)
    for s in range(n):
        rows = pl.ds(pl.multiple_of(base + s * 8, 8), 8)
        parts = []
        for k in range(4):
            at = slice((s * 4 + k) * 8, (s * 4 + k + 1) * 8)
            out = lax.dot_general(
                weight[at], kv_ref[s, k, 1], (((1,), (1,)), ((), ())),
                preferred_element_type=F32,
            )
            o_ref[rows, k * HD : (k + 1) * HD] = out * inverse[at]
            parts.append(logs[at])
        store_side(o_ref, rows, parts)


def core_kernel(
    groups, rows, sub, qt_ref, slot_ref, plen_ref, s_ref, tail_hbm, slot_hbm,
    t_ref, b_ref,
    tail_buf, keys, values, got, out, tail_sem, slot_sem, send1, recv1, send2, recv2, own_sem,
):
    me = lax.axis_index("grp")
    barrier = pltpu.get_barrier_semaphore()

    def offset(i):
        return lax.rem(i * 37, groups)

    def ahead(i):
        return lax.rem(me + offset(i), groups)

    def behind(i):
        return lax.rem(me + groups - offset(i), groups)

    def greet(i, _):
        pl.semaphore_signal(barrier, inc=1, device_id={"grp": ahead(i)}, device_id_type=MESH)
        return 0

    lax.fori_loop(1, groups, greet, 0)

    def block(ref, i):
        return ref.at[pl.ds(pl.multiple_of(i * rows, rows), rows)]

    step = tail_buf.shape[1]
    steps = tail_hbm.shape[0] // step

    def fetch(i):
        slot = lax.rem(i, 2)
        return pltpu.make_async_copy(
            tail_hbm.at[pl.ds(i * step, step)], tail_buf.at[slot], tail_sem.at[slot]
        )

    def tails(i):
        fetch(i).wait()

        @pl.when(i + 1 < steps)
        def _():
            fetch(i + 1).start()

        tail_block(qt_ref, tail_buf.at[lax.rem(i, 2)], t_ref, i * (step * 8))

    heads = keys.shape[0]
    length = keys.shape[2]
    caches = []
    for k in range(heads):
        caches.append(
            pltpu.make_async_copy(slot_hbm.at[0, k, 0], keys.at[k, 0:HD], slot_sem.at[2 * k])
        )
        caches.append(
            pltpu.make_async_copy(slot_hbm.at[0, k, 1], values.at[k, 0:HD], slot_sem.at[2 * k + 1])
        )
    fetch(0).start()
    own_in = pltpu.make_async_copy(block(s_ref, me), block(got, 0), own_sem.at[0])
    own_in.start()
    tails(0)

    def copy_out(i):
        return pltpu.make_async_remote_copy(
            src_ref=block(s_ref, ahead(i)), dst_ref=block(got, i),
            send_sem=send1.at[i], recv_sem=recv1.at[i],
            device_id={"grp": ahead(i)}, device_id_type=MESH,
        )

    def copy_back(i):
        return pltpu.make_async_remote_copy(
            src_ref=block(out, i), dst_ref=block(b_ref, me),
            send_sem=send2.at[i], recv_sem=recv2.at[i],
            device_id={"grp": behind(i)}, device_id_type=MESH,
        )

    def run(first, last, action):
        def body(i, _):
            action(i)
            return 0

        lax.fori_loop(first, last, body, 0)

    slot = slot_ref[...].astype(F32)
    slots = slot.shape[1]
    reqs = plen_ref.shape[1]
    at = iota((1, slots), 1)
    mine = jnp.sum(jnp.where(at == me, slot, 0.0), axis=1, keepdims=True)
    part = jnp.sum(jnp.where((slot == mine) & (at < me), 1.0, 0.0), axis=1, keepdims=True)
    owned = iota((1, reqs), 1).astype(F32) == mine
    tokens = jnp.sum(jnp.where(owned, plen_ref[...].astype(F32), 0.0), axis=1, keepdims=True)
    cached = jnp.minimum(tokens, float(W))
    start = part * float(length)
    index = iota((1, length), 1).astype(F32)
    bias = jnp.where(index < cached - start, 0.0, NEG)
    more = keys.shape[1] - HD
    first = iota((more, length), 0) == 0
    for k in range(heads):
        keys[k, HD:] = jnp.where(first, bias, 0.0).astype(BF16)
        values[k, HD:] = jnp.where(first, 1.0, 0.0).astype(BF16)
    floor0 = cached - float(W) - start

    pl.semaphore_wait(barrier, groups - 1)
    run(1, groups, lambda i: copy_out(i).start())
    for copy in caches:
        copy.start()

    run(1, steps - 1, tails)
    for copy in caches:
        copy.wait()
    own_in.wait()
    near = 384
    per = sub // rows

    def slot_block(b, _):
        run(lax.max(b * per, 1), (b + 1) * per, lambda i: copy_out(i).wait_recv())
        span = pl.ds(pl.multiple_of(b * sub, sub), sub)
        tail = got[span, SIDE:].astype(F32)[:, 0:1]
        token = ((iota((sub, 1), 0) >> 2) & 1).astype(F32)
        floor = tail + token + floor0
        lane = iota((sub, 128), 1)
        logs = []
        for k in range(heads):
            q = got[span, k * HD : k * HD + 128].astype(F32)
            q = jnp.where(lane < HD, q, jnp.where(lane == HD, 1.0, 0.0)).astype(BF16)
            score = jnp.dot(q, keys[k], preferred_element_type=F32)
            head = jnp.where(index[:, :near] > floor, score[:, :near], NEG)
            score = jnp.concatenate([head, score[:, near:]], axis=1)
            top = jnp.max(score, axis=1, keepdims=True)
            weight = jnp.exp2(score - top).astype(BF16)
            res = lax.dot_general(
                weight, values[k], (((1,), (1,)), ((), ())), preferred_element_type=F32
            )
            total = res[:, HD : HD + 1]
            out[span, k * HD : (k + 1) * HD] = (res[:, :HD] * (1.0 / total)).astype(BF16)
            logs.append(top + jnp.log2(total))
        store_side(out, span, logs)

        @pl.when(b > 0)
        def _():
            run(lax.max((b - 1) * per, 1), b * per, lambda i: copy_back(i).start())

        return 0

    blocks = groups // per
    lax.fori_loop(0, blocks, slot_block, 0)
    tails(steps - 1)
    run(max((blocks - 1) * per, 1), groups, lambda i: copy_back(i).start())
    own_out = pltpu.make_async_copy(block(out, 0), block(b_ref, me), own_sem.at[1])
    own_out.start()
    run(1, groups, lambda i: copy_out(i).wait_send())
    run(1, groups, lambda i: copy_back(i).wait())
    own_out.wait()


def core(qt, slot, plen, send, tail_kv, slot_kv, groups):
    rows = send.shape[0] // groups
    sub = min(256, send.shape[0])
    n = tail_kv.shape[0]
    step = 8
    heads = slot_kv.shape[1]
    length = slot_kv.shape[4]
    vmem = pl.BlockSpec(memory_space=pltpu.VMEM)
    hbm = pl.BlockSpec(memory_space=pl.ANY)
    dma = pltpu.SemaphoreType.DMA
    return pl.pallas_call(
        functools.partial(core_kernel, groups, rows, sub),
        in_specs=[vmem, vmem, vmem, hbm, hbm, hbm],
        out_specs=[vmem, hbm],
        out_shape=[
            jax.ShapeDtypeStruct((n * 8, WIDE), F32),
            jax.ShapeDtypeStruct(send.shape, BF16),
        ],
        scratch_shapes=[
            pltpu.VMEM((2, step) + tail_kv.shape[1:], BF16),
            pltpu.VMEM((heads, 128, length), BF16),
            pltpu.VMEM((heads, 128, length), BF16),
            pltpu.VMEM(send.shape, BF16),
            pltpu.VMEM(send.shape, BF16),
            dma((2,)), dma((2 * heads,)),
            dma((groups,)), dma((groups,)), dma((groups,)), dma((groups,)), dma((2,)),
        ],
        compiler_params=pltpu.CompilerParams(
            collective_id=0, has_side_effects=True, vmem_limit_bytes=60 << 20
        ),
        name="core",
    )(qt, slot, plen, send, tail_kv, slot_kv)


def mix_kernel(b_ref, t_ref, qb_ref, own_ref, req_ref, slot_ref, wo_ref, m_ref, mb_ref, att):
    @pl.when(pl.program_id(0) == 0)
    def _():
        n = own_ref.shape[1]
        slots = slot_ref.shape[1]
        rows = 8 * n
        back = slots * 16
        code = sample_codes(to_col(req_ref[...].astype(F32), n), 4.0, n)
        spread = iota((rows, n), 1) == (iota((rows, n), 0) & (n - 1))
        code = jnp.sum(jnp.where(spread, to_row(code, n), 0.0), axis=1, keepdims=True)
        slot = slot_ref[...].astype(F32)
        slot_col = to_col(slot, slots)
        earlier = (slot == slot_col) & (iota((slots, slots), 1) < iota((slots, slots), 0))
        part = jnp.sum(jnp.where(earlier, 1.0, 0.0), axis=1, keepdims=True)
        key = slot_col * 4.0 + part * 2.0
        spread = iota((slots, back), 0) == (iota((slots, back), 1) >> 4)
        key = jnp.sum(jnp.where(spread, key, 0.0), axis=0, keepdims=True)
        key = key + ((iota((1, back), 1) >> 3) & 1).astype(F32)
        same = (iota((rows, back), 0) // n) == (iota((rows, back), 1) & 7)
        code = jnp.where(same, code, -8.0)
        returned = b_ref[...]
        parts = []
        for p in range(2):
            pick = jnp.where(key == code + 2.0 * p, 1.0, 0.0).astype(BF16)
            parts.append(jnp.dot(pick, returned, preferred_element_type=F32))
        r = iota((rows, rows), 0)
        c = iota((rows, rows), 1)
        perm = ((c >> 3) == (r & (n - 1))) & ((c & 7) == (r // n))
        perm = jnp.where(perm, 1.0, 0.0).astype(BF16)
        parts.append(jnp.dot(perm, t_ref[...].astype(BF16), preferred_element_type=F32))

        l = iota((WIDE, 128), 0)
        c = iota((WIDE, 128), 1)
        gather = (l >= SIDE) & (l < SIDE + 12) & (((l - SIDE) & 3) == c)
        gather = jnp.where(gather, 1.0, 0.0).astype(BF16)
        segment = jnp.where((l // HD == c) & (c < 4), 1.0, 0.0)
        logs = [jnp.dot(x.astype(BF16), gather, preferred_element_type=F32) for x in parts]
        logs[1] = jnp.where(parts[1][:, SIDE + 12 : SIDE + 13] > 0.5, logs[1], NEG)
        query = qb_ref[...].astype(F32)
        values = [x for x in parts]
        for u in range(2):
            keys = jnp.concatenate([own_ref[u]] * 8, axis=0)
            s = jnp.dot(
                query * keys, segment, preferred_element_type=F32,
                precision=lax.Precision.HIGHEST,
            )
            if u:
                s = jnp.where(iota(s.shape, 0) >= 4 * n, s, NEG)
            logs.append(s)
            values.append(jnp.concatenate([own_ref[2 + u]] * 8, axis=0))
        top = functools.reduce(jnp.maximum, logs)
        weights = [jnp.exp2(x - top) for x in logs]
        inverse = 1.0 / functools.reduce(jnp.add, weights)
        lane = iota((rows, WIDE), 1)
        out = jnp.zeros((rows, WIDE), F32)
        for w, v in zip(weights, values):
            w = w * inverse
            wide = jnp.broadcast_to(w[:, 3:4], (rows, WIDE))
            for k in (2, 1, 0):
                wide = jnp.where(lane < (k + 1) * HD, w[:, k : k + 1], wide)
            out += wide * v
        out = out.astype(BF16)
        for k in range(4):
            for j in range(4):
                for t in range(2):
                    row = (t * 4 + j) * n
                    att[t * n : (t + 1) * n, (k * 4 + j) * HD : (k * 4 + j + 1) * HD] = out[
                        row : row + n, k * HD : (k + 1) * HD
                    ]

    mixed = jnp.dot(att[...], wo_ref[...], preferred_element_type=F32)
    m_ref[...] = mixed
    mb_ref[...] = mixed.astype(BF16)


def mix(b, t, qb, own, req, slot, wo):
    n = own.shape[1]
    d = wo.shape[1]
    width = 512
    full = lambda a: pl.BlockSpec(a.shape, lambda i: (0,) * a.ndim)
    return pl.pallas_call(
        mix_kernel,
        grid=(d // width,),
        in_specs=[full(a) for a in (b, t, qb, own, req, slot)]
        + [pl.BlockSpec((wo.shape[0], width), lambda i: (0, i))],
        out_specs=[pl.BlockSpec((2 * n, width), lambda i: (0, i))] * 2,
        out_shape=[
            jax.ShapeDtypeStruct((2 * n, d), F32),
            jax.ShapeDtypeStruct((2 * n, d), BF16),
        ],
        scratch_shapes=[pltpu.VMEM((2 * n, wo.shape[0]), BF16)],
        compiler_params=pltpu.CompilerParams(vmem_limit_bytes=60 << 20),
        name="mix",
    )(b, t, qb, own, req, slot, wo)


def finish_kernel(m_ref, mb_ref, x_ref, gain_ref, w_ref, h_ref, s_ref, got, send_sem, recv_sem):
    tp = lax.axis_index("tp")
    partner = {"tp": 1 - tp}
    barrier = pltpu.get_barrier_semaphore()
    pl.semaphore_signal(barrier, inc=1, device_id=partner, device_id_type=MESH)
    pl.semaphore_wait(barrier, 1)
    copy = pltpu.make_async_remote_copy(
        src_ref=mb_ref, dst_ref=got, send_sem=send_sem, recv_sem=recv_sem,
        device_id=partner, device_id_type=MESH,
    )
    copy.start()
    n = x_ref.shape[0]
    d = x_ref.shape[1] // 2
    share = d // 2
    scale = gain_ref[...] * w_ref[...]
    copy.wait()
    mine = pl.multiple_of(tp * share, 128)
    for t in range(2):
        rows = slice(t * n, (t + 1) * n)
        total = (
            x_ref[:, t * d : (t + 1) * d].astype(F32) + m_ref[rows, :] + got[rows, :].astype(F32)
        )
        square = jnp.mean(total * total, axis=-1, keepdims=True)
        score = jnp.sum(total * scale, axis=-1, keepdims=True) * lax.rsqrt(square + EPS)
        s_ref[t : t + 1, :] = to_row(score, n)
        at = pl.multiple_of(tp * share + t * d, 128)
        h_ref[:, t * share : (t + 1) * share] = (
            x_ref[:, pl.ds(at, share)].astype(F32)
            + m_ref[rows, pl.ds(mine, share)]
            + got[rows, pl.ds(mine, share)].astype(F32)
        )


def finish(m, mb, x, gain, w):
    n = x.shape[0]
    d = x.shape[1] // 2
    vmem = pl.BlockSpec(memory_space=pltpu.VMEM)
    return pl.pallas_call(
        finish_kernel,
        in_specs=[vmem] * 5,
        out_specs=[vmem] * 2,
        out_shape=[
            jax.ShapeDtypeStruct((n, d), F32),
            jax.ShapeDtypeStruct((2, n), F32),
        ],
        scratch_shapes=[
            pltpu.VMEM((2 * n, d), BF16),
            pltpu.SemaphoreType.DMA,
            pltpu.SemaphoreType.DMA,
        ],
        compiler_params=pltpu.CompilerParams(collective_id=7, has_side_effects=True),
        name="finish",
    )(m, mb, x, gain, w)


def local(
    hidden_in, prompt_len, slot_req, sample_req, tail_len, slot_kv, tail_kv,
    attn_gain, wqkv, wo, out_gain, score_w,
):
    n, _, d = hidden_in.shape
    groups = lax.axis_size("grp")
    x = hidden_in.reshape(n, 2 * d)
    tail = tail_len.reshape(1, n)
    plen = prompt_len.reshape(1, -1)
    slot = slot_req.reshape(1, -1)
    half = HD // 2
    freq = ROPE_BASE ** (-np.arange(half, dtype=np.float64) / half)
    freq = jnp.asarray(np.concatenate([freq, freq])[None, :], F32)
    req = sample_req.reshape(1, n)
    send, qt, qb, own = qkv(x, req, tail, plen, slot, attn_gain.reshape(1, d), freq, wqkv)
    tails, back = core(qt, slot, plen, send, tail_kv, slot_kv, groups)
    m, mb = mix(back, tails, qb, own, req, slot, wo)
    h, score = finish(m, mb, x, out_gain.reshape(1, d), score_w.reshape(1, d))
    return (h.reshape(n, 2, d // 2), score.T)


def solution(mesh):
    in_specs = (
        P("grp", None, None),
        P(),
        P(),
        P("grp", None),
        P("grp"),
        P("grp", "tp", None, None, None),
        P("grp", "tp", None, None, None),
        P(),
        P(None, "tp"),
        P("tp", None),
        P(),
        P(),
    )
    out_specs = (P("grp", None, "tp"), P("grp", None))
    return jax.shard_map(local, mesh=mesh, in_specs=in_specs, out_specs=out_specs, check_vma=False)
```

```python
import functools

import jax
import jax.numpy as jnp
import numpy as np
from jax import lax
from jax.experimental import pallas as pl
from jax.experimental.pallas import tpu as pltpu
from jax.sharding import PartitionSpec as P

W = 4096
HD = 80
EPS = 1e-05
ROPE_BASE = 10000.0
NEG = -1e30
MESH = pl.DeviceIdType.MESH
F32 = jnp.float32
BF16 = jnp.bfloat16
LOG2E = 1.4426950408889634
SCALE2 = HD**-0.5 * LOG2E
WIDE = 384
SIDE = 320


def iota(shape, dim):
    return lax.broadcasted_iota(jnp.int32, shape, dim)


def to_row(col, size):
    eye = iota((size, size), 0) == iota((size, size), 1)
    return jnp.sum(jnp.where(eye, col, 0.0), axis=0, keepdims=True)


def to_col(row, size):
    eye = iota((size, size), 0) == iota((size, size), 1)
    return jnp.sum(jnp.where(eye, row, 0.0), axis=1, keepdims=True)


def as_row(ref):
    return jnp.concatenate([ref[c : c + 1, :] for c in range(ref.shape[0])], axis=1)


def put(ref, tj, value):
    for c in range(ref.shape[0]):
        ref[c, pl.ds(tj, value.shape[0], stride=8), :] = value[:, c * 128 : (c + 1) * 128]


def take(ref, tj):
    count = ref.shape[1] // 8
    return jnp.concatenate(
        [ref[c, pl.ds(tj, count, stride=8), :] for c in range(ref.shape[0])], axis=1
    )


def joined(ref, rows):
    return jnp.concatenate([ref[c, rows, :] for c in range(ref.shape[0])], axis=1)


def split3(x):
    hi = x.astype(BF16).astype(F32)
    rest = x - hi
    mid = rest.astype(BF16).astype(F32)
    low = (rest - mid).astype(BF16).astype(F32)
    return hi, mid, low


def sample_codes(req, rank_scale, samples):
    req_row = to_row(req, samples)
    shape = (samples, samples)
    before = (req == req_row) & (iota(shape, 1) < iota(shape, 0))
    rank = jnp.sum(jnp.where(before, 1.0, 0.0), axis=1, keepdims=True)
    return req * rank_scale + rank


def store_side(ref, rows, logs):
    n = logs[0].shape[0]
    lane = iota((n, WIDE - SIDE), 1)
    side = jnp.where(lane == 12, 1.0, 0.0)
    for k, value in enumerate(logs):
        for p, term in enumerate(split3(value)):
            side = jnp.where(lane == 4 * p + k, term, side)
    ref[rows, SIDE:] = side.astype(ref.dtype)


def tail_block(q_ref, kv_ref, o_ref, base):
    n = kv_ref.shape[0]
    scores = []
    limits = []
    for s in range(n):
        rows = pl.ds(pl.multiple_of(base + s * 8, 8), 8)
        packed = joined(q_ref, rows)
        limit = packed[:, SIDE : SIDE + 1]
        for k in range(4):
            q = packed[:, k * HD : (k + 1) * HD].astype(BF16)
            scores.append(jnp.dot(q, kv_ref[s, k, 0], preferred_element_type=F32))
            limits.append(limit)
    score = jnp.concatenate(scores, axis=0)
    limit = jnp.concatenate(limits, axis=0)
    at = iota(score.shape, 1).astype(F32)
    score = jnp.where(at < limit, score, NEG)
    top = jnp.max(score, axis=1, keepdims=True)
    weight = jnp.exp2(score - top)
    total = jnp.sum(weight, axis=1, keepdims=True)
    inverse = 1.0 / total
    logs = top + jnp.log2(total)
    weight = weight.astype(BF16)
    for s in range(n):
        rows = pl.ds(pl.multiple_of(base + s * 8, 8), 8)
        parts = []
        outs = []
        for k in range(4):
            at = slice((s * 4 + k) * 8, (s * 4 + k + 1) * 8)
            out = lax.dot_general(
                weight[at], kv_ref[s, k, 1], (((1,), (1,)), ((), ())),
                preferred_element_type=F32,
            )
            outs.append(out * inverse[at])
            parts.append(logs[at])
        lane = iota((8, WIDE - SIDE), 1)
        side = jnp.zeros((8, WIDE - SIDE), F32)
        for k in range(4):
            side = jnp.where(lane == k, parts[k], side)
        value = jnp.concatenate(outs + [side], axis=1)
        for c in range(o_ref.shape[0]):
            o_ref[c, rows, :] = value[:, c * 128 : (c + 1) * 128]


def core_kernel(
    groups, rows, sub, x_ref, req_ref, len_ref, slot_ref, plen_ref, gain_ref, freq_ref,
    wqkv_hbm, tail_hbm, slot_hbm, wo_hbm,
    m_ref, g_ref,
    wqkv, normed, xt, turn, acc, qt_ref, qb_ref, own_ref, s_ref,
    t_ref, b_ref, tail_buf, keys, values, got, out, wo, wide, own_log, home, att, mb,
    tail_sem, slot_sem, send1, recv1, send2, recv2, own_sem, wo_sem, send3, recv3, wq_sem,
):
    me = lax.axis_index("grp")
    barrier = pltpu.get_barrier_semaphore()
    pieces, deep, _ = wqkv.shape

    def project_copy(c):
        at = pl.multiple_of(c * deep, deep)
        return pltpu.make_async_copy(wqkv_hbm.at[pl.ds(at, deep)], wqkv.at[c], wq_sem.at[c])

    for c in range(pieces):
        project_copy(c).start()

    def offset(i):
        return lax.rem(i * 37, groups)

    def ahead(i):
        return lax.rem(me + offset(i), groups)

    def behind(i):
        return lax.rem(me + groups - offset(i), groups)

    def greet(i, _):
        pl.semaphore_signal(barrier, inc=1, device_id={"grp": ahead(i)}, device_id_type=MESH)
        return 0

    lax.fori_loop(1, groups, greet, 0)
    partner = {"tp": 1 - lax.axis_index("tp")}
    pl.semaphore_signal(barrier, inc=1, device_id=partner, device_id_type=MESH)

    def block(ref, i):
        return ref.at[pl.ds(pl.multiple_of(i * rows, rows), rows)]

    step = tail_buf.shape[1]
    steps = tail_hbm.shape[0] // step
    depth = tail_buf.shape[0]
    heads = keys.shape[0]
    length = keys.shape[2]

    def fetch(i):
        slot = lax.rem(i, depth)
        return pltpu.make_async_copy(
            tail_hbm.at[pl.ds(i * step, step)], tail_buf.at[slot], tail_sem.at[slot]
        )

    def tails(i):
        fetch(i).wait()

        @pl.when(i + depth - 1 < steps)
        def _():
            fetch(i + depth - 1).start()

        tail_block(qt_ref, tail_buf.at[lax.rem(i, depth)], t_ref, i * (step * 8))

    caches = []
    for k in range(heads):
        caches.append(
            pltpu.make_async_copy(slot_hbm.at[0, k, 0], keys.at[k, 0:HD], slot_sem.at[2 * k])
        )
        caches.append(
            pltpu.make_async_copy(slot_hbm.at[0, k, 1], values.at[k, 0:HD], slot_sem.at[2 * k + 1])
        )
    n = x_ref.shape[0]
    for t in range(2):
        at = slice(t * n, (t + 1) * n)
        x = x_ref[:, t, :].astype(F32)
        xt[at, :] = x.astype(BF16)
        r = lax.rsqrt(jnp.mean(x * x, axis=-1, keepdims=True) + EPS)
        y = (x * r * as_row(gain_ref)).astype(BF16)
        for c in range(pieces):
            normed[c, at, :] = y[:, c * deep : (c + 1) * deep]
    req = to_col(req_ref[...].astype(F32), n)
    plen = plen_ref[...].astype(F32)
    slot = slot_ref[...].astype(F32)
    slots = slot.shape[1]
    reqs = plen.shape[1]
    owned = req == iota((n, reqs), 1).astype(F32)
    tail = to_col(len_ref[...].astype(F32), n)
    pos = jnp.sum(jnp.where(owned, plen, 0.0), axis=1, keepdims=True) + tail
    angle = jnp.concatenate([pos, pos + 1.0], axis=0) * freq_ref[...]
    half = HD // 2
    sine = jnp.sin(angle)
    turn[0] = jnp.cos(angle)
    turn[1] = jnp.where(iota(sine.shape, 1) < half, -sine, sine)
    acc[...] = jnp.zeros_like(acc)
    own_ref[...] = jnp.zeros_like(own_ref)

    def project(c, _):
        project_copy(c).wait()
        acc[...] += jnp.dot(normed[c], wqkv[c], preferred_element_type=F32)
        return 0

    lax.fori_loop(0, pieces, project, 0)
    for i in range(depth - 1):
        fetch(i).start()

    def rope(u):
        turned = jnp.concatenate([u[:, half:], u[:, :half]], axis=1)
        return u * turn[0] + turned * turn[1]

    for k in range(heads):
        base = k * 6 * HD
        for j in range(4):
            u = (rope(acc[:, base + j * HD : base + (j + 1) * HD]) * SCALE2).astype(BF16)
            for t in range(2):
                row = (t * 4 + j) * n
                qb_ref[row : row + n, k * HD : (k + 1) * HD] = u[t * n : (t + 1) * n]
        fresh = rope(acc[:, base + 4 * HD : base + 5 * HD]).astype(BF16).astype(F32)
        value = acc[:, base + 5 * HD : base + 6 * HD].astype(BF16).astype(F32)
        for t in range(2):
            own_ref[t, :, k * HD : (k + 1) * HD] = fresh[t * n : (t + 1) * n]
            own_ref[2 + t, :, k * HD : (k + 1) * HD] = value[t * n : (t + 1) * n]
    side = jnp.broadcast_to(tail, (n, WIDE - SIDE)).astype(BF16)
    code = to_row(sample_codes(req, 2.0, n), n)
    spread = iota((2 * slots, slots), 1) == (iota((2 * slots, slots), 0) >> 1)
    want = jnp.sum(jnp.where(spread, slot, 0.0), axis=1, keepdims=True) * 2.0
    want = want + (iota((2 * slots, 1), 0) & 1).astype(F32)
    pick = jnp.where(want == code, 1.0, 0.0).astype(BF16)
    for tj in range(8):
        at = slice(tj * n, (tj + 1) * n)
        qb_ref[at, SIDE:] = side
        q = qb_ref[at, :]
        put(qt_ref, tj, q.astype(F32))
        put(wide, tj, jnp.dot(pick, q, preferred_element_type=F32))
    for c in range(3):
        s_ref[:, c * 128 : (c + 1) * 128] = wide[c].astype(BF16)
    own_in = pltpu.make_async_copy(block(s_ref, me), block(got, 0), own_sem.at[0])
    tails(0)

    def copy_out(i):
        return pltpu.make_async_remote_copy(
            src_ref=block(s_ref, ahead(i)), dst_ref=block(got, i),
            send_sem=send1.at[i], recv_sem=recv1.at[i],
            device_id={"grp": ahead(i)}, device_id_type=MESH,
        )

    def copy_back(i):
        return pltpu.make_async_remote_copy(
            src_ref=block(out, i), dst_ref=block(b_ref, me),
            send_sem=send2.at[i], recv_sem=recv2.at[i],
            device_id={"grp": behind(i)}, device_id_type=MESH,
        )

    def run(first, last, action):
        def body(i, _):
            action(i)
            return 0

        lax.fori_loop(first, last, body, 0)

    at = iota((1, slots), 1)
    mine = jnp.sum(jnp.where(at == me, slot, 0.0), axis=1, keepdims=True)
    part = jnp.sum(jnp.where((slot == mine) & (at < me), 1.0, 0.0), axis=1, keepdims=True)
    owned = iota((1, reqs), 1).astype(F32) == mine
    tokens = jnp.sum(jnp.where(owned, plen, 0.0), axis=1, keepdims=True)
    cached = jnp.minimum(tokens, float(W))
    start = part * float(length)
    index = iota((1, length), 1).astype(F32)
    bias = jnp.where(index < cached - start, 0.0, NEG)
    more = keys.shape[1] - HD
    first = iota((more, length), 0) == 0
    for k in range(heads):
        keys[k, HD:] = jnp.where(first, bias, 0.0).astype(BF16)
        values[k, HD:] = jnp.where(first, 1.0, 0.0).astype(BF16)
    floor0 = cached - float(W) - start

    pl.semaphore_wait(barrier, groups)
    own_in.start()
    run(1, groups, lambda i: copy_out(i).start())
    for copy in caches:
        copy.start()

    run(1, steps - 1, tails)
    chunks, _, width = wo.shape
    weights = [
        pltpu.make_async_copy(wo_hbm.at[:, c * width : (c + 1) * width], wo.at[c], wo_sem.at[c])
        for c in range(chunks)
    ]
    for copy in weights:
        copy.start()
    shape = (WIDE, WIDE)
    head_of = iota(shape, 1) // HD
    segment = jnp.where((iota(shape, 0) // HD == head_of) & (head_of < heads), 1.0, 0.0)
    segment = segment.astype(BF16)
    for tj in range(8):
        at = slice(tj * n, (tj + 1) * n)
        query = qb_ref[at, :].astype(F32)
        for u in range(2 if tj >= 4 else 1):
            prod = query * own_ref[u]
            high = prod.astype(BF16)
            low = (prod - high.astype(F32)).astype(BF16)
            own_log[u, at, :] = jnp.dot(high, segment, preferred_element_type=F32) + jnp.dot(
                low, segment, preferred_element_type=F32
            )
    shape = (128, WIDE)
    lane = iota(shape, 0) - (SIDE - 256)
    head_of = iota(shape, 1) // HD
    one_term = jnp.where((lane == head_of) & (head_of < heads), 1.0, 0.0).astype(BF16)
    same = (lane >= 0) & (lane < 12) & ((lane & 3) == head_of)
    terms = jnp.where(same, 1.0, 0.0).astype(BF16)
    code = sample_codes(req, 4.0, n)
    slot_col = to_col(slot, slots)
    earlier = (slot == slot_col) & (iota((slots, slots), 1) < iota((slots, slots), 0))
    key = jnp.sum(jnp.where(earlier, 1.0, 0.0), axis=1, keepdims=True) * 2.0 + slot_col * 4.0
    spread = iota((slots, 2 * slots), 0) == (iota((slots, 2 * slots), 1) >> 1)
    key = jnp.sum(jnp.where(spread, key, 0.0), axis=0, keepdims=True)
    key = key + (iota((1, 2 * slots), 1) & 1).astype(F32)
    code = jnp.concatenate([code, code + 2.0], axis=0)
    pick = jnp.where(key == code, 1.0, 0.0)
    split = jnp.sum(pick[n:], axis=1, keepdims=True) > 0.5
    pick = pick.astype(BF16)
    for copy in caches:
        copy.wait()
    own_in.wait()
    near = 384
    per = sub // rows

    def slot_block(b, _):
        run(lax.max(b * per, 1), (b + 1) * per, lambda i: copy_out(i).wait_recv())
        for h in range(2):
            span = pl.ds(pl.multiple_of(b * sub + h * (sub // 2), sub // 2), sub // 2)
            tail = got[span, SIDE:].astype(F32)[:, 0:1]
            token = ((iota((sub // 2, 1), 0) >> 2) & 1).astype(F32)
            floor = tail + token + floor0
            lane = iota((sub // 2, 96), 1)
            logs = []
            for k in range(heads):
                q = got[span, k * HD : k * HD + 96].astype(F32)
                q = jnp.where(lane < HD, q, jnp.where(lane == HD, 1.0, 0.0)).astype(BF16)
                score = jnp.dot(q, keys[k], preferred_element_type=F32)
                head = jnp.where(index[:, :near] > floor, score[:, :near], NEG)
                score = jnp.concatenate([head, score[:, near:]], axis=1)
                top = jnp.max(score, axis=1, keepdims=True)
                weight = jnp.exp2(score - top).astype(BF16)
                res = lax.dot_general(
                    weight, values[k], (((1,), (1,)), ((), ())), preferred_element_type=F32
                )
                total = res[:, HD : HD + 1]
                out[span, k * HD : (k + 1) * HD] = (res[:, :HD] * (1.0 / total)).astype(BF16)
                logs.append(top + jnp.log2(total))
            store_side(out, span, logs)

        @pl.when(b > 0)
        def _():
            run(lax.max((b - 1) * per, 1), b * per, lambda i: copy_back(i).start())

        return 0

    blocks = groups // per
    lax.fori_loop(0, blocks, slot_block, 0)
    tails(steps - 1)
    run(max((blocks - 1) * per, 1), groups, lambda i: copy_back(i).start())
    own_out = pltpu.make_async_copy(block(out, 0), block(b_ref, me), own_sem.at[1])
    own_out.start()

    for tj in range(8):
        at = slice(tj * n, (tj + 1) * n)
        tail = take(t_ref, tj)
        spread = [
            jnp.dot(x.astype(BF16), one_term, preferred_element_type=F32)
            for x in split3(tail[:, 256:])
        ]
        logs = [functools.reduce(jnp.add, spread), own_log[0, at, :]]
        parts = [tail, own_ref[2]]
        if tj >= 4:
            logs.append(own_log[1, at, :])
            parts.append(own_ref[3])
        top = functools.reduce(jnp.maximum, logs)
        shares = [jnp.exp2(x - top) for x in logs]
        home[at, :] = functools.reduce(jnp.add, [w * v for w, v in zip(shares, parts)])
        own_log[0, at, :] = top
        own_log[1, at, :] = functools.reduce(jnp.add, shares)

    run(1, groups, lambda i: copy_back(i).wait_recv())
    own_out.wait()
    for c in range(3):
        wide[c] = b_ref[:, c * 128 : (c + 1) * 128].astype(F32)
    for tj in range(8):
        at = slice(tj * n, (tj + 1) * n)
        both = jnp.dot(pick, take(wide, tj).astype(BF16), preferred_element_type=F32)
        logs = jnp.dot(both[:, 256:].astype(BF16), terms, preferred_element_type=F32)
        log1 = logs[:n]
        log2 = jnp.where(split, logs[n:], NEG)
        top = own_log[0, at, :]
        peak = jnp.maximum(top, jnp.maximum(log1, log2))
        w0 = jnp.exp2(top - peak)
        w1 = jnp.exp2(log1 - peak)
        w2 = jnp.exp2(log2 - peak)
        res = home[at, :] * w0 + both[:n] * w1 + both[n:] * w2
        res = (res * (1.0 / (own_log[1, at, :] * w0 + w1 + w2))).astype(BF16)
        t, j = divmod(tj, 4)
        for k in range(heads):
            att[t * n : (t + 1) * n, (k * 4 + j) * HD : (k * 4 + j + 1) * HD] = res[
                :, k * HD : (k + 1) * HD
            ]

    def give(c):
        cols = slice(c * width, (c + 1) * width)
        return pltpu.make_async_remote_copy(
            src_ref=mb.at[:, cols], dst_ref=g_ref.at[:, cols],
            send_sem=send3.at[c], recv_sem=recv3.at[c],
            device_id=partner, device_id_type=MESH,
        )

    for c in range(chunks):
        weights[c].wait()
        mixed = jnp.dot(att[...], wo[c], preferred_element_type=F32)
        cols = slice(c * width, (c + 1) * width)
        m_ref[:, cols] = mixed + xt[:, cols].astype(F32)
        mb[:, c * width : (c + 1) * width] = mixed.astype(BF16)
        if c:
            give(c - 1).start()
    run(1, groups, lambda i: copy_out(i).wait_send())
    run(1, groups, lambda i: copy_back(i).wait_send())
    give(chunks - 1).start()
    for c in range(chunks):
        give(c).wait()


def core(x, req, tail, slot, plen, gain, freq, wqkv, tail_kv, slot_kv, wo, groups):
    n = tail_kv.shape[0]
    rows = 16
    send = jax.ShapeDtypeStruct((groups * rows, WIDE), BF16)
    sub = min(256, groups * rows)
    step = 8
    heads = slot_kv.shape[1]
    length = slot_kv.shape[4]
    depth, d = wo.shape
    chunks = 5
    vmem = pl.BlockSpec(memory_space=pltpu.VMEM)
    hbm = pl.BlockSpec(memory_space=pl.ANY)
    dma = pltpu.SemaphoreType.DMA
    return pl.pallas_call(
        functools.partial(core_kernel, groups, rows, sub),
        in_specs=[vmem] * 7 + [hbm] * 4,
        out_specs=[vmem, hbm],
        out_shape=[
            jax.ShapeDtypeStruct((2 * n, d), F32),
            jax.ShapeDtypeStruct((2 * n, d), BF16),
        ],
        scratch_shapes=[
            pltpu.VMEM((chunks, d // chunks, wqkv.shape[1]), BF16),
            pltpu.VMEM((chunks, 2 * n, d // chunks), BF16),
            pltpu.VMEM((2 * n, d), BF16),
            pltpu.VMEM((2, 2 * n, HD), F32),
            pltpu.VMEM((2 * n, wqkv.shape[1]), F32),
            pltpu.VMEM((3, n * 8, 128), F32),
            pltpu.VMEM((n * 8, WIDE), BF16),
            pltpu.VMEM((4, n, WIDE), F32),
            pltpu.VMEM(send.shape, BF16),
            pltpu.VMEM((3, n * 8, 128), F32),
            pltpu.VMEM(send.shape, BF16),
            pltpu.VMEM((4, step) + tail_kv.shape[1:], BF16),
            pltpu.VMEM((heads, 96, length), BF16),
            pltpu.VMEM((heads, 96, length), BF16),
            pltpu.VMEM(send.shape, BF16),
            pltpu.VMEM(send.shape, BF16),
            pltpu.VMEM((chunks, depth, d // chunks), BF16),
            pltpu.VMEM((3, send.shape[0], 128), F32),
            pltpu.VMEM((2, n * 8, WIDE), F32),
            pltpu.VMEM((n * 8, WIDE), F32),
            pltpu.VMEM((2 * n, depth), BF16),
            pltpu.VMEM((2 * n, d), BF16),
            dma((4,)), dma((2 * heads,)),
            dma((groups,)), dma((groups,)), dma((groups,)), dma((groups,)), dma((2,)),
            dma((chunks,)), dma((chunks,)), dma((chunks,)), dma((chunks,)),
        ],
        compiler_params=pltpu.CompilerParams(
            collective_id=0, has_side_effects=True, vmem_limit_bytes=60 << 20
        ),
        name="core",
    )(x, req, tail, slot, plen, gain, freq, wqkv, tail_kv, slot_kv, wo)


def finish_kernel(m_ref, g_ref, gain_ref, w_ref, h_ref, s_ref):
    n = m_ref.shape[0] // 2
    d = m_ref.shape[1]
    share = d // 2
    tp = lax.axis_index("tp")
    scale = as_row(gain_ref) * as_row(w_ref)
    mine = pl.multiple_of(tp * share, 128)
    for t in range(2):
        rows = slice(t * n, (t + 1) * n)
        total = m_ref[rows, :] + g_ref[rows, :].astype(F32)
        square = jnp.mean(total * total, axis=-1, keepdims=True)
        score = jnp.sum(total * scale, axis=-1, keepdims=True) * lax.rsqrt(square + EPS)
        s_ref[t : t + 1, :] = to_row(score, n)
        h_ref[:, t, :] = m_ref[rows, pl.ds(mine, share)] + g_ref[rows, pl.ds(mine, share)].astype(F32)


def finish(m, g, gain, w):
    n = m.shape[0] // 2
    d = m.shape[1]
    vmem = pl.BlockSpec(memory_space=pltpu.VMEM)
    return pl.pallas_call(
        finish_kernel,
        in_specs=[vmem] * 4,
        out_specs=[vmem] * 2,
        out_shape=[
            jax.ShapeDtypeStruct((n, 2, d // 2), F32),
            jax.ShapeDtypeStruct((2, n), F32),
        ],
        name="finish",
    )(m, g, gain, w)


def local(
    hidden_in, prompt_len, slot_req, sample_req, tail_len, slot_kv, tail_kv,
    attn_gain, wqkv, wo, out_gain, score_w,
):
    n, _, d = hidden_in.shape
    groups = lax.axis_size("grp")
    tail = tail_len.reshape(1, n)
    plen = prompt_len.reshape(1, -1)
    slot = slot_req.reshape(1, -1)
    half = HD // 2
    freq = ROPE_BASE ** (-np.arange(half, dtype=np.float64) / half)
    freq = jnp.asarray(np.concatenate([freq, freq])[None, :], F32)
    req = sample_req.reshape(1, n)
    req = sample_req.reshape(1, n)
    fold = lambda v: v.reshape(d // 128, 128)
    m, g = core(
        hidden_in, req, tail, slot, plen, fold(attn_gain), freq,
        wqkv, tail_kv, slot_kv, wo, groups,
    )
    h, score = finish(m, g, fold(out_gain), fold(score_w))
    return (h, score.T)


def solution(mesh):
    in_specs = (
        P("grp", None, None),
        P(),
        P(),
        P("grp", None),
        P("grp"),
        P("grp", "tp", None, None, None),
        P("grp", "tp", None, None, None),
        P(),
        P(None, "tp"),
        P("tp", None),
        P(),
        P(),
    )
    out_specs = (P("grp", None, "tp"), P("grp", None))
    return jax.shard_map(local, mesh=mesh, in_specs=in_specs, out_specs=out_specs, check_vma=False)
```
